1024 devices in a mesh: occ: 32 (over z_lo, x, core), vir: 32 (over z_hi, y).
Axes of the slice: x: 8, y: 8, z: 8 (z_hi: 4, z_lo: 2; z = z_hi * 2 + z_lo), core: 2. Of those that a mesh axis runs over, the one named last changes fastest.
Arguments:
- amplitudes: bfloat16 [131072, 256], P(('vir', 'occ')), may hold values from -6 to 6
- pair_irrep: int32 [1024], P('vir'), may hold values from 0 to 7
- integrals: bfloat16 [32, 8, 128, 4096], P('vir', None, None, 'occ'), may hold values from -0.375 to 0.375
- panel_blocks: int32 [32, 8], P('vir'), may hold values from 0 to 7, each once within a row
- panel_owner: int32 [2], replicated, may hold values from 0 to 31
Outputs:
- ladder: bfloat16 [131072, 4096], P('vir', 'occ')
The draws below stay inside these ranges and needn't reach their ends.
Inputs may be any that keep to these rules, and one draw needn't show every extreme that they name: Each row of panel_blocks names every irrep once.
All inputs are finite; a program needn't handle non-finite values.
Results may differ from the reference program's by a relative error of at most 0.001.
Values may be sent and summed in bfloat16 or wider, within the bound.
No kernel may reach another device: no remote copies, remote signals or barrier semaphores. Data moves between devices by JAX's collectives and lax.ppermute only.
A program may use at most 32 MiB of HBM per device.

```python
import jax
import jax.numpy as jnp
from jax import lax

IRREPS = 8
STEPS = 2
PAIR_DEV = 128
KB = 128
TILES = 1024
PAIRS = 131072
COLS = 4096
N_VIR = 32


def place_ends(values, own_key, low, largest):
    shape = values.shape
    place = [jax.random.randint(jax.random.fold_in(own_key, axis), (), 0, shape[axis]) for axis in range(len(shape))]
    values = values.at[tuple(place)].set(low)
    longest = shape.index(max(shape))
    place[longest] = (place[longest] + 1) % shape[longest]
    return values.at[tuple(place)].set(largest)


def steps_of(stream_key, shape, pieces, smallest, high):
    loudness, own = 1.0, jax.random.fold_in(stream_key, 6)
    for position, blocks in pieces:
        heights = jnp.exp(jax.random.uniform(jax.random.fold_in(own, position), (blocks,), jnp.float32, smallest / len(pieces), high / len(pieces)))
        loudness = loudness * jnp.repeat(heights, shape[position] // blocks).reshape([-1 if axis == position else 1 for axis in range(len(shape))])
    return loudness


def scatter_about(key, dims, deviation, reach, split=(), kind=jnp.bfloat16):
    array = deviation * jax.random.normal(key, dims, jnp.float32)
    if split:
        array = array * steps_of(key, dims, split, -0.22, 0.18)
    return jnp.clip(array, -reach, reach).astype(kind)


def setup_inputs(seed: int = 0) -> dict:
    streams_of = jax.random.split(jax.random.key(seed), 6)
    return {
        "amplitudes": scatter_about(streams_of[0], (PAIRS, STEPS * KB), 1.0, 6.0, ((0, 1024),)),
        "pair_irrep": place_ends(jax.random.randint(streams_of[1], (TILES,), 0, IRREPS), jax.random.fold_in(streams_of[1], 1), 0, IRREPS - 1).astype(jnp.int32),
        "integrals": scatter_about(streams_of[2], (N_VIR, IRREPS, KB, COLS), (STEPS * KB) ** -0.5, 0.375, ((0, 32), (3, 32))),
        "panel_blocks": jax.vmap(lambda own: jax.random.permutation(own, IRREPS))(jax.random.split(streams_of[3], N_VIR)).reshape((N_VIR, IRREPS)).astype(jnp.int32),
        "panel_owner": jax.random.randint(streams_of[4], (STEPS,), 0, N_VIR).astype(jnp.int32),
    }


def reference(amplitudes, pair_irrep, integrals, panel_blocks, panel_owner):
    irrep_ids = jnp.arange(IRREPS, dtype=jnp.int32)
    ordered = []
    for step_index in range(STEPS):
        blocks = panel_blocks[panel_owner[step_index]]
        matches = blocks[None, :] == irrep_ids[:, None]
        slot_ids = jnp.sum(jnp.where(matches, irrep_ids[None, :], 0), axis=1).astype(jnp.int32)
        ordered.append(jnp.take(integrals[panel_owner[step_index]], slot_ids, axis=0))
    amp_tiles = amplitudes.reshape(TILES, PAIR_DEV, STEPS * KB)

    def tile_ladder(inputs):
        tile_rows, irrep = inputs
        weights = jnp.concatenate(
            [lax.dynamic_index_in_dim(one_panel, irrep, 0, keepdims=False) for one_panel in ordered], axis=0)
        return jnp.dot(tile_rows, weights, preferred_element_type=jnp.float32).astype(jnp.bfloat16)

    ladder = lax.map(tile_ladder, (amp_tiles, pair_irrep))
    return ladder.reshape(PAIRS, COLS)
```

```python
import jax
import jax.numpy as jnp
from jax import lax
from jax.experimental import pallas as pl
from jax.experimental.pallas import tpu as pltpu
from jax.sharding import Mesh, PartitionSpec as P

OCC = ("zl", "x", "core")
VIR = ("zh", "y")
N_VIR = 32


def order_kernel(blocks_ref, panel_ref, out_ref):
    for slot in range(panel_ref.shape[0]):
        out_ref[blocks_ref[slot]] = panel_ref[slot]


def irrep_order(panel, blocks):
    return pl.pallas_call(
        order_kernel,
        out_shape=jax.ShapeDtypeStruct(panel.shape, panel.dtype),
        in_specs=[
            pl.BlockSpec(memory_space=pltpu.SMEM),
            pl.BlockSpec(memory_space=pltpu.VMEM),
        ],
        out_specs=pl.BlockSpec(memory_space=pltpu.VMEM),
        name="irrep_order",
    )(blocks, panel)


def pick_and_copy(pieces, owners):
    chosen = jnp.concatenate(
        [lax.dynamic_slice_in_dim(pieces, owners[step], 1, 0) for step in range(owners.shape[0])], axis=1
    )
    return jnp.broadcast_to(chosen, pieces.shape[:1] + chosen.shape[1:])


def ladder_kernel(label_ref, half_ref, own_ref, other_ref, weight_ref, out_ref):
    per_block = own_ref.shape[0]
    first = pl.program_id(0) * per_block
    total = pl.num_programs(0) * per_block
    quarters = weight_ref.shape[0] // 8
    for member in range(per_block):
        for half, tiles_ref in ((half_ref[0], own_ref), (1 - half_ref[0], other_ref)):
            irrep = label_ref[half * total + first + member]
            weights = weight_ref[pl.ds(irrep * quarters, quarters)]
            rows = weights.shape[1] // 2
            weights = jnp.concatenate(
                [weights[:, :rows].reshape(-1, weights.shape[2]),
                 weights[:, rows:].reshape(-1, weights.shape[2])], axis=0)
            out_ref[half, member] = jnp.dot(
                tiles_ref[member], weights, preferred_element_type=jnp.float32
            ).astype(out_ref.dtype)


def contract(own, other, labels, half, weights, per_block):
    members, rows, depth = own.shape
    cols = weights.shape[2]
    tiles = pl.BlockSpec((per_block, rows, depth), lambda i, *scalars: (i, 0, 0))
    out = pl.pallas_call(
        ladder_kernel,
        out_shape=jax.ShapeDtypeStruct((2, members, rows, cols), jnp.bfloat16),
        grid_spec=pltpu.PrefetchScalarGridSpec(
            num_scalar_prefetch=2,
            grid=(members // per_block,),
            in_specs=[tiles, tiles, pl.BlockSpec(weights.shape, lambda i, *scalars: (0, 0, 0))],
            out_specs=pl.BlockSpec((2, per_block, rows, cols), lambda i, *scalars: (0, i, 0, 0)),
        ),
        name="ladder",
    )(labels, half, own, other, weights)
    return out.reshape(2 * members * rows, cols)


def per_device(amplitudes, pair_irrep, integrals, panel_blocks, panel_owner):
    rows, depth = amplitudes.shape
    cols = integrals.shape[-1]
    partner = lax.ppermute(amplitudes, "zl", [(0, 1), (1, 0)])
    own = lax.all_gather(amplitudes, ("x", "core"), axis=0, tiled=True)
    other = lax.all_gather(partner, ("x", "core"), axis=0, tiled=True)
    ordered = irrep_order(integrals[0], panel_blocks[0])
    pieces = lax.all_to_all(ordered.reshape(N_VIR, -1, cols), VIR, 0, 0, tiled=True)
    copies = pick_and_copy(pieces, panel_owner)
    weights = lax.all_to_all(copies, VIR, 0, 0, tiled=True)
    half = lax.axis_index("zl").reshape(1)
    tiles = lambda amps: amps.reshape(-1, rows, depth)
    return contract(tiles(own), tiles(other), pair_irrep, half, weights, 8)


def solution(mesh):
    fine = Mesh(mesh.devices.reshape(2, 8, 2, 4, 8), OCC + VIR)
    return jax.shard_map(
        per_device,
        mesh=fine,
        in_specs=(
            P(VIR + OCC, None),
            P(VIR),
            P(VIR, None, None, OCC),
            P(VIR, None),
            P(),
        ),
        out_specs=P(VIR, OCC),
        check_vma=False,
    )
```

```python
import jax
import jax.numpy as jnp
from jax import lax
from jax.experimental import pallas as pl
from jax.experimental.pallas import tpu as pltpu
from jax.sharding import Mesh, PartitionSpec as P


OCC = ("zl", "x", "core")
VIR = ("zh", "y")
N_VIR = 32
N_X = 8
IRREPS = 8


def order_kernel(blocks_ref, panel_ref, out_ref):
    for slot in range(panel_ref.shape[0]):
        out_ref[blocks_ref[slot]] = panel_ref[slot]


def irrep_order(panel, blocks):
    return pl.pallas_call(
        order_kernel,
        out_shape=pltpu.VMEM(panel.shape, panel.dtype),
        in_specs=[
            pl.BlockSpec(memory_space=pltpu.SMEM),
            pl.BlockSpec(memory_space=pltpu.VMEM),
        ],
        out_specs=pl.BlockSpec(memory_space=pltpu.VMEM),
        name="irrep_order",
    )(blocks, panel)


def pick_kernel(owner_ref, pieces_ref, out_ref):
    count, rows, cols = pieces_ref.shape
    for step in range(out_ref.shape[1] // rows):
        out_ref[:, step * rows:(step + 1) * rows, :] = jnp.broadcast_to(
            pieces_ref[pl.ds(owner_ref[step], 1)], (count, rows, cols)
        )


def pick_and_copy(pieces, owners):
    count, rows, cols = pieces.shape
    return pl.pallas_call(
        pick_kernel,
        out_shape=pltpu.VMEM((count, owners.shape[0] * rows, cols), pieces.dtype),
        in_specs=[
            pl.BlockSpec(memory_space=pltpu.SMEM),
            pl.BlockSpec(memory_space=pltpu.VMEM),
        ],
        out_specs=pl.BlockSpec(memory_space=pltpu.VMEM),
    )(owners, pltpu.with_memory_space_constraint(pieces, pltpu.VMEM))


BLOCK = ((-1, 0), (0, 0), (1, 0))
FAR = ((-4, 0), (-3, 0), (-2, 0), (2, 0), (3, 0))
OTHER_BLOCK = tuple((x, 1) for x, _ in BLOCK)
OTHER_FAR = tuple((x, 1) for x, _ in FAR)
NEAR = BLOCK + FAR + OTHER_BLOCK


def ladder_kernel(groups, piece_ref, here_ref, side_ref, *refs):
    held_refs, refs = refs[:len(groups)], refs[len(groups):]
    weight_ref, out_ref, done_ref, sems, in_sems = refs[:5]
    tiles_refs = refs[5:]
    quarters = weight_ref.shape[0] // IRREPS
    copies = []
    arrivals = [
        pltpu.make_async_copy(held_ref, tiles_ref, in_sems.at[group])
        for group, (held_ref, tiles_ref) in enumerate(zip(held_refs, tiles_refs))
    ]
    for arrival in arrivals:
        arrival.start()
    for (core_step, places), tiles_ref, arrival in zip(groups, tiles_refs, arrivals):
        arrival.wait()
        for index, (x_step, zl_step) in enumerate(places):
            zl = lax.rem(here_ref[0] + zl_step, 2)
            x = lax.rem(here_ref[1] + x_step + N_X, N_X)
            core = lax.rem(side_ref[0] + core_step, 2)
            tile = (zl * N_X + x) * 2 + core
            weights = weight_ref[pl.ds(piece_ref[tile], quarters)]
            rows = weights.shape[1] // 2
            weights = jnp.concatenate(
                [weights[:, :rows].reshape(-1, weights.shape[2]),
                 weights[:, rows:].reshape(-1, weights.shape[2])], axis=0)
            slot = len(copies)
            done_ref[slot] = jnp.dot(
                tiles_ref[index], weights, preferred_element_type=jnp.float32
            ).astype(done_ref.dtype)
            copy = pltpu.make_async_copy(done_ref.at[slot], out_ref.at[tile], sems.at[slot])
            copy.start()
            copies.append(copy)
    for copy in copies:
        copy.wait()


def contract(groups, arrays, first_piece, here, side, weights):
    rows = arrays[0].shape[1]
    cols = weights.shape[2]
    count = sum(array.shape[0] for array in arrays)
    vmem, smem = pl.BlockSpec(memory_space=pltpu.VMEM), pl.BlockSpec(memory_space=pltpu.SMEM)
    operands = [pltpu.with_memory_space_constraint(array, pltpu.HBM) for array in arrays]
    operands.append(pltpu.with_memory_space_constraint(weights, pltpu.VMEM))
    out = pl.pallas_call(
        lambda *refs: ladder_kernel(groups, *refs),
        out_shape=jax.ShapeDtypeStruct((count, rows, cols), jnp.bfloat16),
        in_specs=[smem, smem, smem] + [pl.BlockSpec(memory_space=pltpu.HBM)] * len(arrays) + [vmem],
        out_specs=pl.BlockSpec(memory_space=pl.ANY),
        scratch_shapes=[
            pltpu.VMEM((count, rows, cols), jnp.bfloat16),
            pltpu.SemaphoreType.DMA((count,)),
            pltpu.SemaphoreType.DMA((len(arrays),)),
            *(pltpu.VMEM(array.shape, array.dtype) for array in arrays),
        ],
        name="ladder",
    )(first_piece, here, side, *operands)
    return out.reshape(count * rows, cols)


def shift(array, axis, size, step):
    return lax.ppermute(array, axis, [(index, (index + step) % size) for index in range(size)])


def per_device(amplitudes, pair_irrep, integrals, panel_blocks, panel_owner):
    cols = integrals.shape[-1]
    left = shift(amplitudes, "x", N_X, 1)
    right = shift(amplitudes, "x", N_X, -1)
    ordered = irrep_order(integrals[0], panel_blocks[0])
    pieces = lax.all_to_all(ordered.reshape(N_VIR, -1, cols), VIR, 0, 0, tiled=True)
    block = jnp.stack([left, amplitudes, right])
    up = shift(block, "x", N_X, 3)
    down = shift(block, "x", N_X, -3)
    other_block = shift(block, "zl", 2, 1)
    here = jnp.stack([lax.axis_index("zl"), lax.axis_index("x")])
    copies = pick_and_copy(pieces, panel_owner)
    weights = lax.all_to_all(copies, VIR, 0, 0, tiled=True)
    side = jnp.arange(16, dtype=jnp.int32) + lax.axis_index("core")
    far = jnp.concatenate([up, down[:2]])
    other_far = shift(far, "zl", 2, 1)
    near = jnp.concatenate([block, up, down[:2], other_block])
    share_near = shift(near, "core", 2, 1)
    first_piece = pair_irrep * (N_VIR // IRREPS)
    share_far = shift(other_far, "core", 2, 1)
    groups = ((0, NEAR), (1, NEAR), (0, OTHER_FAR), (1, OTHER_FAR))
    return contract(
        groups, (near, share_near, other_far, share_far), first_piece, here, side, weights)


def solution(mesh):
    fine = Mesh(mesh.devices.reshape(2, 8, 2, 4, 8), OCC + VIR)
    return jax.shard_map(
        per_device,
        mesh=fine,
        in_specs=(
            P(VIR + OCC, None),
            P(VIR),
            P(VIR, None, None, OCC),
            P(VIR, None),
            P(),
        ),
        out_specs=P(VIR, OCC),
        check_vma=False,
    )
```

```python
import jax
import jax.numpy as jnp
from jax import lax
from jax.experimental import pallas as pl
from jax.experimental.pallas import tpu as pltpu
from jax.sharding import Mesh, PartitionSpec as P


OCC = ("zl", "x", "core")
VIR = ("zh", "y")
N_VIR = 32
N_X = 8
IRREPS = 8


def order_kernel(blocks_ref, panel_ref, out_ref):
    for slot in range(panel_ref.shape[0]):
        out_ref[blocks_ref[slot]] = panel_ref[slot]


def irrep_order(panel, blocks):
    return pl.pallas_call(
        order_kernel,
        out_shape=pltpu.VMEM(panel.shape, panel.dtype),
        in_specs=[
            pl.BlockSpec(memory_space=pltpu.SMEM),
            pl.BlockSpec(memory_space=pltpu.VMEM),
        ],
        out_specs=pl.BlockSpec(memory_space=pltpu.VMEM),
        name="irrep_order",
    )(blocks, panel)


def pick_kernel(owner_ref, pieces_ref, out_ref):
    count, rows, cols = pieces_ref.shape
    for step in range(out_ref.shape[1] // rows):
        out_ref[:, step * rows:(step + 1) * rows, :] = jnp.broadcast_to(
            pieces_ref[pl.ds(owner_ref[step], 1)], (count, rows, cols)
        )


def pick_and_copy(pieces, owners):
    count, rows, cols = pieces.shape
    return pl.pallas_call(
        pick_kernel,
        out_shape=pltpu.VMEM((count, owners.shape[0] * rows, cols), pieces.dtype),
        in_specs=[
            pl.BlockSpec(memory_space=pltpu.SMEM),
            pl.BlockSpec(memory_space=pltpu.VMEM),
        ],
        out_specs=pl.BlockSpec(memory_space=pltpu.VMEM),
    )(owners, pltpu.with_memory_space_constraint(pieces, pltpu.VMEM))


NEAR = ((-1, 0), (-1, 1), (0, 0), (0, 1), (1, 0), (1, 1))
UP = ((-4, 0), (-3, 0), (-3, 1), (-2, 0), (-2, 1))
DOWN = ((2, 0), (2, 1), (3, 0), (3, 1), (4, 1))


def ladder_kernel(groups, piece_ref, here_ref, side_ref, *refs):
    held_refs, refs = refs[:len(groups)], refs[len(groups):]
    weight_ref, out_ref, done_ref, sems, in_sems = refs[:5]
    tiles_refs = refs[5:]
    quarters = weight_ref.shape[0] // IRREPS
    copies = []
    arrivals = [
        pltpu.make_async_copy(held_ref, tiles_ref, in_sems.at[group])
        for group, (held_ref, tiles_ref) in enumerate(zip(held_refs, tiles_refs))
    ]
    for arrival in arrivals:
        arrival.start()
    for (core_step, places), tiles_ref, arrival in zip(groups, tiles_refs, arrivals):
        arrival.wait()
        for index, (x_step, zl_step) in enumerate(places):
            zl = lax.rem(here_ref[0] + zl_step, 2)
            x = lax.rem(here_ref[1] + x_step + N_X, N_X)
            core = lax.rem(side_ref[0] + core_step, 2)
            tile = (zl * N_X + x) * 2 + core
            weights = weight_ref[pl.ds(piece_ref[tile], quarters)]
            rows = weights.shape[1] // 2
            weights = jnp.concatenate(
                [weights[:, :rows].reshape(-1, weights.shape[2]),
                 weights[:, rows:].reshape(-1, weights.shape[2])], axis=0)
            slot = len(copies)
            done_ref[slot] = jnp.dot(
                tiles_ref[index], weights, preferred_element_type=jnp.float32
            ).astype(done_ref.dtype)
            copy = pltpu.make_async_copy(done_ref.at[slot], out_ref.at[tile], sems.at[slot])
            copy.start()
            copies.append(copy)
    for copy in copies:
        copy.wait()


def contract(groups, arrays, first_piece, here, side, weights):
    rows = arrays[0].shape[1]
    cols = weights.shape[2]
    count = sum(array.shape[0] for array in arrays)
    vmem, smem = pl.BlockSpec(memory_space=pltpu.VMEM), pl.BlockSpec(memory_space=pltpu.SMEM)
    operands = [pltpu.with_memory_space_constraint(array, pltpu.HBM) for array in arrays]
    operands.append(pltpu.with_memory_space_constraint(weights, pltpu.VMEM))
    out = pl.pallas_call(
        lambda *refs: ladder_kernel(groups, *refs),
        out_shape=jax.ShapeDtypeStruct((count, rows, cols), jnp.bfloat16),
        in_specs=[smem, smem, smem] + [pl.BlockSpec(memory_space=pltpu.HBM)] * len(arrays) + [vmem],
        out_specs=pl.BlockSpec(memory_space=pl.ANY),
        scratch_shapes=[
            pltpu.VMEM((count, rows, cols), jnp.bfloat16),
            pltpu.SemaphoreType.DMA((count,)),
            pltpu.SemaphoreType.DMA((len(arrays),)),
            *(pltpu.VMEM(array.shape, array.dtype) for array in arrays),
        ],
        name="ladder",
    )(first_piece, here, side, *operands)
    return out.reshape(count * rows, cols)


def shift(array, axis, size, step):
    return lax.ppermute(array, axis, [(index, (index + step) % size) for index in range(size)])


def per_device(amplitudes, pair_irrep, integrals, panel_blocks, panel_owner):
    cols = integrals.shape[-1]
    partner = shift(amplitudes, "zl", 2, 1)
    ordered = irrep_order(integrals[0], panel_blocks[0])
    pieces = lax.all_to_all(ordered.reshape(N_VIR, -1, cols), VIR, 0, 0, tiled=True)
    pair = jnp.stack([amplitudes, partner])
    left = shift(pair, "x", N_X, 1)
    right = shift(pair, "x", N_X, -1)
    here = jnp.stack([lax.axis_index("zl"), lax.axis_index("x")])
    copies = pick_and_copy(pieces, panel_owner)
    for_up = jnp.concatenate([left[:1], pair, right])
    for_down = jnp.concatenate([left, pair, right[1:]])
    up = shift(for_up, "x", N_X, 3)
    down = shift(for_down, "x", N_X, -3)
    weights = lax.all_to_all(copies, VIR, 0, 0, tiled=True)
    near = jnp.concatenate([left, pair, right])
    share_near = shift(near, "core", 2, 1)
    side = jnp.arange(16, dtype=jnp.int32) + lax.axis_index("core")
    share_up = shift(up, "core", 2, 1)
    share_down = shift(down, "core", 2, 1)
    first_piece = pair_irrep * (N_VIR // IRREPS)
    groups = ((0, NEAR), (1, NEAR), (0, UP), (0, DOWN), (1, UP), (1, DOWN))
    arrays = (near, share_near, up, down, share_up, share_down)
    return contract(groups, arrays, first_piece, here, side, weights)


def solution(mesh):
    fine = Mesh(mesh.devices.reshape(2, 8, 2, 4, 8), OCC + VIR)
    return jax.shard_map(
        per_device,
        mesh=fine,
        in_specs=(
            P(VIR + OCC, None),
            P(VIR),
            P(VIR, None, None, OCC),
            P(VIR, None),
            P(),
        ),
        out_specs=P(VIR, OCC),
        check_vma=False,
    )
```

```python
import jax
import jax.numpy as jnp
from jax import lax
from jax.experimental import pallas as pl
from jax.experimental.pallas import tpu as pltpu
from jax.sharding import Mesh, PartitionSpec as P


OCC = ("zl", "x", "core")
VIR = ("zh", "y")
N_VIR = 32
N_X = 8
IRREPS = 8


def order_kernel(blocks_ref, panel_ref, out_ref):
    for slot in range(panel_ref.shape[0]):
        out_ref[blocks_ref[slot]] = panel_ref[slot]


def irrep_order(panel, blocks):
    return pl.pallas_call(
        order_kernel,
        out_shape=pltpu.VMEM(panel.shape, panel.dtype),
        in_specs=[
            pl.BlockSpec(memory_space=pltpu.SMEM),
            pl.BlockSpec(memory_space=pltpu.VMEM),
        ],
        out_specs=pl.BlockSpec(memory_space=pltpu.VMEM),
        name="irrep_order",
    )(blocks, panel)


def pick_kernel(owner_ref, pieces_ref, out_ref):
    count, rows, cols = pieces_ref.shape
    for step in range(out_ref.shape[1] // rows):
        out_ref[:, step * rows:(step + 1) * rows, :] = jnp.broadcast_to(
            pieces_ref[pl.ds(owner_ref[step], 1)], (count, rows, cols)
        )


def pick_and_copy(pieces, owners):
    count, rows, cols = pieces.shape
    return pl.pallas_call(
        pick_kernel,
        out_shape=pltpu.VMEM((count, owners.shape[0] * rows, cols), pieces.dtype),
        in_specs=[
            pl.BlockSpec(memory_space=pltpu.SMEM),
            pl.BlockSpec(memory_space=pltpu.VMEM),
        ],
        out_specs=pl.BlockSpec(memory_space=pltpu.VMEM),
    )(owners, pltpu.with_memory_space_constraint(pieces, pltpu.VMEM))


TILES = tuple((x, zl) for x in (-1, 0, 1, 4, -3, -2, 2, 3) for zl in (0, 1))


def ladder_kernel(groups, piece_ref, here_ref, side_ref, *refs):
    held_refs, refs = refs[:len(groups)], refs[len(groups):]
    weight_ref, out_ref, done_ref, sems, in_sems = refs[:5]
    tiles_refs = refs[5:]
    quarters = weight_ref.shape[0] // IRREPS
    copies = []
    arrivals = [
        pltpu.make_async_copy(held_ref, tiles_ref, in_sems.at[group])
        for group, (held_ref, tiles_ref) in enumerate(zip(held_refs, tiles_refs))
    ]
    for arrival in arrivals:
        arrival.start()
    for (core_step, places), tiles_ref, arrival in zip(groups, tiles_refs, arrivals):
        arrival.wait()
        for index, (x_step, zl_step) in enumerate(places):
            zl = lax.rem(here_ref[0] + zl_step, 2)
            x = lax.rem(here_ref[1] + x_step + N_X, N_X)
            core = lax.rem(side_ref[0] + core_step, 2)
            tile = (zl * N_X + x) * 2 + core
            weights = weight_ref[pl.ds(piece_ref[tile], quarters)]
            rows = weights.shape[1] // 2
            weights = jnp.concatenate(
                [weights[:, :rows].reshape(-1, weights.shape[2]),
                 weights[:, rows:].reshape(-1, weights.shape[2])], axis=0)
            slot = len(copies)
            done_ref[slot] = jnp.dot(
                tiles_ref[index], weights, preferred_element_type=jnp.float32
            ).astype(done_ref.dtype)
            copy = pltpu.make_async_copy(done_ref.at[slot], out_ref.at[tile], sems.at[slot])
            copy.start()
            copies.append(copy)
    for copy in copies:
        copy.wait()


def contract(groups, arrays, first_piece, here, side, weights):
    rows = arrays[0].shape[1]
    cols = weights.shape[2]
    count = sum(array.shape[0] for array in arrays)
    vmem, smem = pl.BlockSpec(memory_space=pltpu.VMEM), pl.BlockSpec(memory_space=pltpu.SMEM)
    operands = [pltpu.with_memory_space_constraint(array, pltpu.HBM) for array in arrays]
    operands.append(pltpu.with_memory_space_constraint(weights, pltpu.VMEM))
    out = pl.pallas_call(
        lambda *refs: ladder_kernel(groups, *refs),
        out_shape=jax.ShapeDtypeStruct((count, rows, cols), jnp.bfloat16),
        in_specs=[smem, smem, smem] + [pl.BlockSpec(memory_space=pltpu.HBM)] * len(arrays) + [vmem],
        out_specs=pl.BlockSpec(memory_space=pl.ANY),
        scratch_shapes=[
            pltpu.VMEM((count, rows, cols), jnp.bfloat16),
            pltpu.SemaphoreType.DMA((count,)),
            pltpu.SemaphoreType.DMA((len(arrays),)),
            *(pltpu.VMEM(array.shape, array.dtype) for array in arrays),
        ],
        name="ladder",
    )(first_piece, here, side, *operands)
    return out.reshape(count * rows, cols)


def shift(array, axis, size, step):
    return lax.ppermute(array, axis, [(index, (index + step) % size) for index in range(size)])


def per_device(amplitudes, pair_irrep, integrals, panel_blocks, panel_owner):
    cols = integrals.shape[-1]
    partner = shift(amplitudes, "zl", 2, 1)
    ordered = irrep_order(integrals[0], panel_blocks[0])
    pieces = lax.all_to_all(ordered.reshape(N_VIR, -1, cols), VIR, 0, 0, tiled=True)
    pair = jnp.stack([amplitudes, partner])
    left = shift(pair, "x", N_X, 1)
    right = shift(pair, "x", N_X, -1)
    opposite = shift(pair, "x", N_X, 4)
    here = jnp.stack([lax.axis_index("zl"), lax.axis_index("x")])
    copies = pick_and_copy(pieces, panel_owner)
    up = shift(jnp.concatenate([left, pair]), "x", N_X, 2)
    down = shift(jnp.concatenate([pair, right]), "x", N_X, -2)
    weights = lax.all_to_all(copies, VIR, 0, 0, tiled=True)
    side = jnp.arange(16, dtype=jnp.int32) + lax.axis_index("core")
    mine = jnp.concatenate([left, pair, right, opposite, up, down])
    theirs = shift(mine, "core", 2, 1)
    first_piece = pair_irrep * (N_VIR // IRREPS)
    groups = ((0, TILES), (1, TILES))
    return contract(groups, (mine, theirs), first_piece, here, side, weights)


def solution(mesh):
    fine = Mesh(mesh.devices.reshape(2, 8, 2, 4, 8), OCC + VIR)
    return jax.shard_map(
        per_device,
        mesh=fine,
        in_specs=(
            P(VIR + OCC, None),
            P(VIR),
            P(VIR, None, None, OCC),
            P(VIR, None),
            P(),
        ),
        out_specs=P(VIR, OCC),
        check_vma=False,
    )
```

```python
import jax
import jax.numpy as jnp
from jax import lax
from jax.experimental import pallas as pl
from jax.experimental.pallas import tpu as pltpu
from jax.sharding import Mesh, PartitionSpec as P


OCC = ("zl", "x", "core")
VIR = ("zh", "y")
N_VIR = 32
N_X = 8
IRREPS = 8


def order_kernel(blocks_ref, panel_ref, out_ref, sems):
    copies = [
        pltpu.make_async_copy(panel_ref.at[slot], out_ref.at[blocks_ref[slot]], sems.at[slot])
        for slot in range(panel_ref.shape[0])
    ]
    for copy in copies:
        copy.start()
    for copy in copies:
        copy.wait()


def irrep_order(panel, blocks):
    return pl.pallas_call(
        order_kernel,
        out_shape=pltpu.VMEM(panel.shape, panel.dtype),
        in_specs=[
            pl.BlockSpec(memory_space=pltpu.SMEM),
            pl.BlockSpec(memory_space=pltpu.HBM),
        ],
        out_specs=pl.BlockSpec(memory_space=pltpu.VMEM),
        scratch_shapes=[pltpu.SemaphoreType.DMA((panel.shape[0],))],
        name="irrep_order",
    )(blocks, panel)


def pick_kernel(owner_ref, pieces_ref, out_ref):
    count, rows, cols = pieces_ref.shape
    for step in range(out_ref.shape[1] // rows):
        out_ref[:, step * rows:(step + 1) * rows, :] = jnp.broadcast_to(
            pieces_ref[pl.ds(owner_ref[step], 1)], (count, rows, cols)
        )


def pick_and_copy(pieces, owners):
    count, rows, cols = pieces.shape
    return pl.pallas_call(
        pick_kernel,
        out_shape=pltpu.VMEM((count, owners.shape[0] * rows, cols), pieces.dtype),
        in_specs=[
            pl.BlockSpec(memory_space=pltpu.SMEM),
            pl.BlockSpec(memory_space=pltpu.VMEM),
        ],
        out_specs=pl.BlockSpec(memory_space=pltpu.VMEM),
    )(owners, pltpu.with_memory_space_constraint(pieces, pltpu.VMEM))


HERE, OPPOSITE, MINE, THEIRS = (0,), (4,), (1, 3, 2), (-1, -3, -2)


def ladder_kernel(groups, piece_ref, here_ref, side_ref, *refs):
    held_refs, refs = refs[:len(groups) - 1], refs[len(groups) - 1:]
    last_ref, weight_ref, out_ref, done_ref, sems, in_sems = refs[:6]
    tiles_refs = refs[6:]
    quarters = weight_ref.shape[0] // IRREPS
    copies = []
    arrivals = [
        pltpu.make_async_copy(held_ref, tiles_ref, in_sems.at[group])
        for group, (held_ref, tiles_ref) in enumerate(zip(held_refs, tiles_refs))
    ]
    for arrival in arrivals:
        arrival.start()
    side = 2 * side_ref[0] - 1
    for group, (steps, tiles_ref) in enumerate(zip(groups, (*tiles_refs, last_ref))):
        if group < len(arrivals):
            arrivals[group].wait()
        for index in range(tiles_ref.shape[0]):
            core, zl = index % 4 // 2, index % 2
            x = lax.rem(here_ref[0] + steps[index // 4] * side + N_X, N_X)
            tile = (zl * N_X + x) * 2 + core
            weights = weight_ref[pl.ds(piece_ref[tile], quarters)]
            rows = weights.shape[1] // 2
            weights = jnp.concatenate(
                [weights[:, :rows].reshape(-1, weights.shape[2]),
                 weights[:, rows:].reshape(-1, weights.shape[2])], axis=0)
            slot = len(copies)
            done_ref[slot] = jnp.dot(
                tiles_ref[index], weights, preferred_element_type=jnp.float32
            ).astype(done_ref.dtype)
            copy = pltpu.make_async_copy(done_ref.at[slot], out_ref.at[tile], sems.at[slot])
            copy.start()
            copies.append(copy)
    for copy in copies:
        copy.wait()


def contract(groups, arrays, first_piece, here, side, weights):
    rows = arrays[0].shape[1]
    cols = weights.shape[2]
    count = sum(array.shape[0] for array in arrays)
    vmem, smem = pl.BlockSpec(memory_space=pltpu.VMEM), pl.BlockSpec(memory_space=pltpu.SMEM)
    *arrays, last = arrays
    operands = [pltpu.with_memory_space_constraint(array, pltpu.HBM) for array in arrays]
    operands += [pltpu.with_memory_space_constraint(array, pltpu.VMEM) for array in (last, weights)]
    out = pl.pallas_call(
        lambda *refs: ladder_kernel(groups, *refs),
        out_shape=jax.ShapeDtypeStruct((count, rows, cols), jnp.bfloat16),
        in_specs=[smem, smem, smem] + [pl.BlockSpec(memory_space=pltpu.HBM)] * len(arrays) + [vmem] * 2,
        out_specs=pl.BlockSpec(memory_space=pl.ANY),
        scratch_shapes=[
            pltpu.VMEM((count, rows, cols), jnp.bfloat16),
            pltpu.SemaphoreType.DMA((count,)),
            pltpu.SemaphoreType.DMA((len(arrays),)),
            *(pltpu.VMEM(array.shape, array.dtype) for array in arrays),
        ],
        name="ladder",
    )(first_piece, here, side, *operands)
    return out.reshape(count * rows, cols)


def away(array, step):
    pairs = []
    for x in range(N_X):
        pairs.append((2 * x, 2 * ((x + step) % N_X)))
        pairs.append((2 * x + 1, 2 * ((x - step) % N_X) + 1))
    return lax.ppermute(array, ("x", "core"), pairs)


def per_device(amplitudes, pair_irrep, integrals, panel_blocks, panel_owner):
    cols = integrals.shape[-1]
    ordered = irrep_order(integrals[0], panel_blocks[0])
    pieces = lax.all_to_all(ordered.reshape(N_VIR, -1, cols), VIR, 0, 0, tiled=True)
    pair = lax.all_gather(amplitudes[None], "zl", axis=0, tiled=True)
    chip = lax.all_gather(pair, "core", axis=0, tiled=True)
    beside = away(chip, 1)
    here = jnp.stack([lax.axis_index("x"), lax.axis_index("zl")])
    copies = pick_and_copy(pieces, panel_owner)
    wide = away(jnp.concatenate([beside, chip]), 2)
    weights = lax.all_to_all(copies, VIR, 0, 0, tiled=True)
    side = jnp.arange(16, dtype=jnp.int32) + lax.axis_index("core")
    opposite = away(wide[:4], 1)
    mine = jnp.concatenate([beside, wide])
    theirs = lax.ppermute(mine, "core", [(0, 1), (1, 0)])
    first_piece = pair_irrep * (N_VIR // IRREPS)
    groups = (HERE, MINE, OPPOSITE, THEIRS)
    arrays = (chip, mine, opposite, theirs)
    return contract(groups, arrays, first_piece, here, side, weights)


def solution(mesh):
    fine = Mesh(mesh.devices.reshape(2, 8, 2, 4, 8), OCC + VIR)
    return jax.shard_map(
        per_device,
        mesh=fine,
        in_specs=(
            P(VIR + OCC, None),
            P(VIR),
            P(VIR, None, None, OCC),
            P(VIR, None),
            P(),
        ),
        out_specs=P(VIR, OCC),
        check_vma=False,
    )
```

```python
import jax
import jax.numpy as jnp
from jax import lax
from jax.experimental import pallas as pl
from jax.experimental.pallas import tpu as pltpu
from jax.sharding import Mesh, PartitionSpec as P


OCC = ("zl", "x", "core")
VIR = ("zh", "y")
N_VIR = 32
N_X = 8
IRREPS = 8


def order_kernel(blocks_ref, panel_ref, out_ref):
    for slot in range(panel_ref.shape[0]):
        out_ref[blocks_ref[slot]] = panel_ref[slot]


def irrep_order(panel, blocks):
    return pl.pallas_call(
        order_kernel,
        out_shape=pltpu.VMEM(panel.shape, panel.dtype),
        in_specs=[
            pl.BlockSpec(memory_space=pltpu.SMEM),
            pl.BlockSpec(memory_space=pltpu.VMEM),
        ],
        out_specs=pl.BlockSpec(memory_space=pltpu.VMEM),
        name="irrep_order",
    )(blocks, panel)


def pick_kernel(owner_ref, pieces_ref, out_ref):
    count, rows, cols = pieces_ref.shape
    for step in range(out_ref.shape[1] // rows):
        out_ref[:, step * rows:(step + 1) * rows, :] = jnp.broadcast_to(
            pieces_ref[pl.ds(owner_ref[step], 1)], (count, rows, cols)
        )


def pick_and_copy(pieces, owners):
    count, rows, cols = pieces.shape
    return pl.pallas_call(
        pick_kernel,
        out_shape=pltpu.VMEM((count, owners.shape[0] * rows, cols), pieces.dtype),
        in_specs=[
            pl.BlockSpec(memory_space=pltpu.SMEM),
            pl.BlockSpec(memory_space=pltpu.VMEM),
        ],
        out_specs=pl.BlockSpec(memory_space=pltpu.VMEM),
    )(owners, pltpu.with_memory_space_constraint(pieces, pltpu.VMEM))


HERE, NEXT, WIDE, OPPOSITE = (0,), (1,), (3, 2), (4,)
OTHER_NEXT, OTHER_WIDE = (-1,), (-3, -2)


def ladder_kernel(groups, first_ref, second_ref, here_ref, side_ref, *refs):
    held_refs, refs = refs[:len(groups) - 1], refs[len(groups) - 1:]
    last_ref, weight_ref, out_ref, done_ref, sems, in_sems = refs[:6]
    tiles_refs = refs[6:]
    quarters = weight_ref.shape[0] // IRREPS
    copies = []
    arrivals = [
        pltpu.make_async_copy(held_ref, tiles_ref, in_sems.at[group])
        for group, (held_ref, tiles_ref) in enumerate(zip(held_refs, tiles_refs))
    ]
    for arrival in arrivals:
        arrival.start()
    side = 2 * side_ref[0] - 1
    for group, (steps, tiles_ref) in enumerate(zip(groups, (*tiles_refs, last_ref))):
        if group < len(arrivals):
            arrivals[group].wait()
        for index in range(tiles_ref.shape[0]):
            core, zl = index % 4 // 2, index % 2
            x = lax.rem((second_ref if zl else here_ref)[0] + steps[index // 4] * side + N_X, N_X)
            tile = (zl * N_X + x) * 2 + core
            weights = weight_ref[pl.ds(first_ref[tile], quarters)]
            rows = weights.shape[1] // 2
            weights = jnp.concatenate(
                [weights[:, :rows].reshape(-1, weights.shape[2]),
                 weights[:, rows:].reshape(-1, weights.shape[2])], axis=0)
            slot = len(copies)
            done_ref[slot] = jnp.dot(
                tiles_ref[index], weights, preferred_element_type=jnp.float32
            ).astype(done_ref.dtype)
            copy = pltpu.make_async_copy(done_ref.at[slot], out_ref.at[tile], sems.at[slot])
            copy.start()
            copies.append(copy)
    for copy in copies:
        copy.wait()


def contract(groups, arrays, first_piece, second, here, side, weights):
    rows = arrays[0].shape[1]
    cols = weights.shape[2]
    count = sum(array.shape[0] for array in arrays)
    vmem, smem = pl.BlockSpec(memory_space=pltpu.VMEM), pl.BlockSpec(memory_space=pltpu.SMEM)
    *arrays, last = arrays
    operands = [pltpu.with_memory_space_constraint(array, pltpu.HBM) for array in arrays]
    operands += [pltpu.with_memory_space_constraint(array, pltpu.VMEM) for array in (last, weights)]
    out = pl.pallas_call(
        lambda *refs: ladder_kernel(groups, *refs),
        out_shape=jax.ShapeDtypeStruct((count, rows, cols), jnp.bfloat16),
        in_specs=[smem] * 4 + [pl.BlockSpec(memory_space=pltpu.HBM)] * len(arrays) + [vmem] * 2,
        out_specs=pl.BlockSpec(memory_space=pl.ANY),
        scratch_shapes=[
            pltpu.VMEM((count, rows, cols), jnp.bfloat16),
            pltpu.SemaphoreType.DMA((count,)),
            pltpu.SemaphoreType.DMA((len(arrays),)),
            *(pltpu.VMEM(array.shape, array.dtype) for array in arrays),
        ],
        name="ladder",
    )(first_piece, second, here, side, *operands)
    return out.reshape(count * rows, cols)


def away(array, step):
    pairs = []
    for x in range(N_X):
        pairs.append((2 * x, 2 * ((x + step) % N_X)))
        pairs.append((2 * x + 1, 2 * ((x - step) % N_X) + 1))
    return lax.ppermute(array, ("x", "core"), pairs)


def per_device(amplitudes, pair_irrep, integrals, panel_blocks, panel_owner):
    cols = integrals.shape[-1]
    ordered = irrep_order(integrals[0], panel_blocks[0])
    pieces = lax.all_to_all(ordered.reshape(N_VIR, -1, cols), VIR, 0, 0, tiled=True)
    pair = lax.all_gather(amplitudes[None], "zl", axis=0, tiled=True)
    chip = lax.all_gather(pair, "core", axis=0, tiled=True)
    beside = away(chip, 1)
    here = jnp.stack([lax.axis_index("x"), lax.axis_index("zl")])
    copies = pick_and_copy(pieces, panel_owner)
    weights = lax.all_to_all(copies, VIR, 0, 0, tiled=True)
    side = jnp.arange(16, dtype=jnp.int32) + lax.axis_index("core")
    wide = away(jnp.concatenate([beside, chip]), 2)
    other_beside = lax.ppermute(beside, "core", [(0, 1), (1, 0)])
    second = jnp.arange(24, dtype=jnp.int32) + lax.axis_index("x")
    opposite = away(wide[:4], 1)
    other_wide = lax.ppermute(wide, "core", [(0, 1), (1, 0)])
    first_piece = pair_irrep * (N_VIR // IRREPS)
    groups = (HERE, NEXT, OTHER_NEXT, WIDE, OPPOSITE, OTHER_WIDE)
    arrays = (chip, beside, other_beside, wide, opposite, other_wide)
    return contract(groups, arrays, first_piece, second, here, side, weights)


def solution(mesh):
    fine = Mesh(mesh.devices.reshape(2, 8, 2, 4, 8), OCC + VIR)
    return jax.shard_map(
        per_device,
        mesh=fine,
        in_specs=(
            P(VIR + OCC, None),
            P(VIR),
            P(VIR, None, None, OCC),
            P(VIR, None),
            P(),
        ),
        out_specs=P(VIR, OCC),
        check_vma=False,
    )
```

```python
import jax
import jax.numpy as jnp
from jax import lax
from jax.experimental import pallas as pl
from jax.experimental.pallas import tpu as pltpu
from jax.sharding import Mesh, PartitionSpec as P


OCC = ("zl", "x", "core")
VIR = ("zh", "y")
N_VIR = 32
N_X = 8
IRREPS = 8


def order_kernel(blocks_ref, panel_ref, out_ref):
    for slot in range(panel_ref.shape[0]):
        out_ref[blocks_ref[slot]] = panel_ref[slot]


def irrep_order(panel, blocks):
    return pl.pallas_call(
        order_kernel,
        out_shape=pltpu.VMEM(panel.shape, panel.dtype),
        in_specs=[
            pl.BlockSpec(memory_space=pltpu.SMEM),
            pl.BlockSpec(memory_space=pltpu.VMEM),
        ],
        out_specs=pl.BlockSpec(memory_space=pltpu.VMEM),
        name="irrep_order",
    )(blocks, panel)


def pick_kernel(owner_ref, pieces_ref, out_ref):
    count, rows, cols = pieces_ref.shape
    for step in range(out_ref.shape[1] // rows):
        out_ref[:, step * rows:(step + 1) * rows, :] = jnp.broadcast_to(
            pieces_ref[pl.ds(owner_ref[step], 1)], (count, rows, cols)
        )


def pick_and_copy(pieces, owners):
    count, rows, cols = pieces.shape
    return pl.pallas_call(
        pick_kernel,
        out_shape=pltpu.VMEM((count, owners.shape[0] * rows, cols), pieces.dtype),
        in_specs=[
            pl.BlockSpec(memory_space=pltpu.SMEM),
            pl.BlockSpec(memory_space=pltpu.VMEM),
        ],
        out_specs=pl.BlockSpec(memory_space=pltpu.VMEM),
    )(owners, pltpu.with_memory_space_constraint(pieces, pltpu.VMEM))


HERE, OPPOSITE, MINE, THEIRS = (0,), (4,), (1, 3, 2), (-1, -3, -2)


def ladder_kernel(groups, piece_ref, here_ref, side_ref, *refs):
    held_refs, refs = refs[:len(groups) - 1], refs[len(groups) - 1:]
    last_ref, weight_ref, out_ref, done_ref, sems, in_sems = refs[:6]
    tiles_refs = refs[6:]
    quarters = weight_ref.shape[0] // IRREPS
    copies = []
    arrivals = [
        pltpu.make_async_copy(held_ref, tiles_ref, in_sems.at[group])
        for group, (held_ref, tiles_ref) in enumerate(zip(held_refs, tiles_refs))
    ]
    for arrival in arrivals:
        arrival.start()
    side = 2 * side_ref[0] - 1
    for group, (steps, tiles_ref) in enumerate(zip(groups, (*tiles_refs, last_ref))):
        if group < len(arrivals):
            arrivals[group].wait()
        for index in range(tiles_ref.shape[0]):
            core, zl = index % 4 // 2, lax.rem(here_ref[1] + index % 2, 2)
            x = lax.rem(here_ref[0] + steps[index // 4] * side + N_X, N_X)
            tile = (zl * N_X + x) * 2 + core
            weights = weight_ref[pl.ds(piece_ref[tile], quarters)]
            rows = weights.shape[1] // 2
            weights = jnp.concatenate(
                [weights[:, :rows].reshape(-1, weights.shape[2]),
                 weights[:, rows:].reshape(-1, weights.shape[2])], axis=0)
            slot = len(copies)
            done_ref[slot] = jnp.dot(
                tiles_ref[index], weights, preferred_element_type=jnp.float32
            ).astype(done_ref.dtype)
            copy = pltpu.make_async_copy(done_ref.at[slot], out_ref.at[tile], sems.at[slot])
            copy.start()
            copies.append(copy)
    for copy in copies:
        copy.wait()


def contract(groups, arrays, first_piece, here, side, weights):
    rows = arrays[0].shape[1]
    cols = weights.shape[2]
    count = sum(array.shape[0] for array in arrays)
    vmem, smem = pl.BlockSpec(memory_space=pltpu.VMEM), pl.BlockSpec(memory_space=pltpu.SMEM)
    *arrays, last = arrays
    operands = [pltpu.with_memory_space_constraint(array, pltpu.HBM) for array in arrays]
    operands += [pltpu.with_memory_space_constraint(array, pltpu.VMEM) for array in (last, weights)]
    out = pl.pallas_call(
        lambda *refs: ladder_kernel(groups, *refs),
        out_shape=jax.ShapeDtypeStruct((count, rows, cols), jnp.bfloat16),
        in_specs=[smem, smem, smem] + [pl.BlockSpec(memory_space=pltpu.HBM)] * len(arrays) + [vmem] * 2,
        out_specs=pl.BlockSpec(memory_space=pl.ANY),
        scratch_shapes=[
            pltpu.VMEM((count, rows, cols), jnp.bfloat16),
            pltpu.SemaphoreType.DMA((count,)),
            pltpu.SemaphoreType.DMA((len(arrays),)),
            *(pltpu.VMEM(array.shape, array.dtype) for array in arrays),
        ],
        name="ladder",
    )(first_piece, here, side, *operands)
    return out.reshape(count * rows, cols)


def away(array, step):
    pairs = []
    for x in range(N_X):
        pairs.append((2 * x, 2 * ((x + step) % N_X)))
        pairs.append((2 * x + 1, 2 * ((x - step) % N_X) + 1))
    return lax.ppermute(array, ("x", "core"), pairs)


def per_device(amplitudes, pair_irrep, integrals, panel_blocks, panel_owner):
    cols = integrals.shape[-1]
    partner = lax.ppermute(amplitudes, "zl", [(0, 1), (1, 0)])
    ordered = irrep_order(integrals[0], panel_blocks[0])
    pieces = lax.all_to_all(ordered.reshape(N_VIR, -1, cols), VIR, 0, 0, tiled=True)
    pair = jnp.stack([amplitudes, partner])
    chip = lax.all_gather(pair, "core", axis=0, tiled=True)
    beside = away(chip, 1)
    here = jnp.stack([lax.axis_index("x"), lax.axis_index("zl")])
    copies = pick_and_copy(pieces, panel_owner)
    wide = away(jnp.concatenate([beside, chip]), 2)
    weights = lax.all_to_all(copies, VIR, 0, 0, tiled=True)
    side = jnp.arange(16, dtype=jnp.int32) + lax.axis_index("core")
    opposite = away(wide[:4], 1)
    mine = jnp.concatenate([beside, wide])
    theirs = lax.ppermute(mine, "core", [(0, 1), (1, 0)])
    first_piece = pair_irrep * (N_VIR // IRREPS)
    groups = (HERE, MINE, OPPOSITE, THEIRS)
    arrays = (chip, mine, opposite, theirs)
    return contract(groups, arrays, first_piece, here, side, weights)


def solution(mesh):
    fine = Mesh(mesh.devices.reshape(2, 8, 2, 4, 8), OCC + VIR)
    return jax.shard_map(
        per_device,
        mesh=fine,
        in_specs=(
            P(VIR + OCC, None),
            P(VIR),
            P(VIR, None, None, OCC),
            P(VIR, None),
            P(),
        ),
        out_specs=P(VIR, OCC),
        check_vma=False,
    )
```

```python
import jax
import jax.numpy as jnp
from jax import lax
from jax.experimental import pallas as pl
from jax.experimental.pallas import tpu as pltpu
from jax.sharding import Mesh, PartitionSpec as P


OCC = ("zl", "x", "core")
VIR = ("zh", "y")
N_VIR = 32
N_X = 8
IRREPS = 8


def order_kernel(blocks_ref, panel_ref, out_ref):
    for slot in range(panel_ref.shape[0]):
        out_ref[blocks_ref[slot]] = panel_ref[slot]


def irrep_order(panel, blocks):
    return pl.pallas_call(
        order_kernel,
        out_shape=pltpu.VMEM(panel.shape, panel.dtype),
        in_specs=[
            pl.BlockSpec(memory_space=pltpu.SMEM),
            pl.BlockSpec(memory_space=pltpu.VMEM),
        ],
        out_specs=pl.BlockSpec(memory_space=pltpu.VMEM),
        name="irrep_order",
    )(blocks, panel)


def pick_kernel(owner_ref, pieces_ref, out_ref):
    count, rows, cols = pieces_ref.shape
    for step in range(out_ref.shape[1] // rows):
        out_ref[:, step * rows:(step + 1) * rows, :] = jnp.broadcast_to(
            pieces_ref[pl.ds(owner_ref[step], 1)], (count, rows, cols)
        )


def pick_and_copy(pieces, owners):
    count, rows, cols = pieces.shape
    return pl.pallas_call(
        pick_kernel,
        out_shape=pltpu.VMEM((count, owners.shape[0] * rows, cols), pieces.dtype),
        in_specs=[
            pl.BlockSpec(memory_space=pltpu.SMEM),
            pl.BlockSpec(memory_space=pltpu.VMEM),
        ],
        out_specs=pl.BlockSpec(memory_space=pltpu.VMEM),
    )(owners, pltpu.with_memory_space_constraint(pieces, pltpu.VMEM))


HERE, OPPOSITE, MINE, THEIRS = (0,), (4,), (1, 2, 3), (-1, -2, -3)


def ladder_kernel(groups, piece_ref, here_ref, side_ref, *refs):
    held_refs, refs = refs[:len(groups) - 1], refs[len(groups) - 1:]
    last_ref, weight_ref, out_ref, done_ref, sems, in_sems = refs[:6]
    tiles_refs = refs[6:]
    quarters = weight_ref.shape[0] // IRREPS
    copies = []
    arrivals = [
        pltpu.make_async_copy(held_ref, tiles_ref, in_sems.at[group])
        for group, (held_ref, tiles_ref) in enumerate(zip(held_refs, tiles_refs))
    ]
    for arrival in arrivals:
        arrival.start()
    side = 2 * side_ref[0] - 1
    for group, (steps, tiles_ref) in enumerate(zip(groups, (*tiles_refs, last_ref))):
        if group < len(arrivals):
            arrivals[group].wait()
        for index in range(tiles_ref.shape[0]):
            core, zl = index % 4 // 2, lax.rem(here_ref[1] + index % 2, 2)
            x = lax.rem(here_ref[0] + steps[index // 4] * side + N_X, N_X)
            tile = (zl * N_X + x) * 2 + core
            weights = weight_ref[pl.ds(piece_ref[tile], quarters)]
            rows = weights.shape[1] // 2
            weights = jnp.concatenate(
                [weights[:, :rows].reshape(-1, weights.shape[2]),
                 weights[:, rows:].reshape(-1, weights.shape[2])], axis=0)
            slot = len(copies)
            done_ref[slot] = jnp.dot(
                tiles_ref[index], weights, preferred_element_type=jnp.float32
            ).astype(done_ref.dtype)
            copy = pltpu.make_async_copy(done_ref.at[slot], out_ref.at[tile], sems.at[slot])
            copy.start()
            copies.append(copy)
    for copy in copies:
        copy.wait()


def contract(groups, arrays, first_piece, here, side, weights):
    rows = arrays[0].shape[1]
    cols = weights.shape[2]
    count = sum(array.shape[0] for array in arrays)
    vmem, smem = pl.BlockSpec(memory_space=pltpu.VMEM), pl.BlockSpec(memory_space=pltpu.SMEM)
    *arrays, last = arrays
    operands = [pltpu.with_memory_space_constraint(array, pltpu.HBM) for array in arrays]
    operands += [pltpu.with_memory_space_constraint(array, pltpu.VMEM) for array in (last, weights)]
    out = pl.pallas_call(
        lambda *refs: ladder_kernel(groups, *refs),
        out_shape=jax.ShapeDtypeStruct((count, rows, cols), jnp.bfloat16),
        in_specs=[smem, smem, smem] + [pl.BlockSpec(memory_space=pltpu.HBM)] * len(arrays) + [vmem] * 2,
        out_specs=pl.BlockSpec(memory_space=pl.ANY),
        scratch_shapes=[
            pltpu.VMEM((count, rows, cols), jnp.bfloat16),
            pltpu.SemaphoreType.DMA((count,)),
            pltpu.SemaphoreType.DMA((len(arrays),)),
            *(pltpu.VMEM(array.shape, array.dtype) for array in arrays),
        ],
        name="ladder",
    )(first_piece, here, side, *operands)
    return out.reshape(count * rows, cols)


def away(array, step):
    pairs = []
    for x in range(N_X):
        pairs.append((2 * x, 2 * ((x + step) % N_X)))
        pairs.append((2 * x + 1, 2 * ((x - step) % N_X) + 1))
    return lax.ppermute(array, ("x", "core"), pairs)


def per_device(amplitudes, pair_irrep, integrals, panel_blocks, panel_owner):
    cols = integrals.shape[-1]
    partner = lax.ppermute(amplitudes, "zl", [(0, 1), (1, 0)])
    ordered = irrep_order(integrals[0], panel_blocks[0])
    pieces = lax.all_to_all(ordered.reshape(N_VIR, -1, cols), VIR, 0, 0, tiled=True)
    pair = jnp.stack([amplitudes, partner])
    chip = lax.all_gather(pair, "core", axis=0, tiled=True)
    beside = away(chip, 1)
    two = away(chip, 2)
    three = away(chip, 3)
    here = jnp.stack([lax.axis_index("x"), lax.axis_index("zl")])
    copies = pick_and_copy(pieces, panel_owner)
    weights = lax.all_to_all(copies, VIR, 0, 0, tiled=True)
    side = jnp.arange(16, dtype=jnp.int32) + lax.axis_index("core")
    opposite = away(three, 1)
    mine = jnp.concatenate([beside, two, three])
    theirs = lax.ppermute(mine, "core", [(0, 1), (1, 0)])
    first_piece = pair_irrep * (N_VIR // IRREPS)
    groups = (HERE, MINE, OPPOSITE, THEIRS)
    arrays = (chip, mine, opposite, theirs)
    return contract(groups, arrays, first_piece, here, side, weights)


def solution(mesh):
    fine = Mesh(mesh.devices.reshape(2, 8, 2, 4, 8), OCC + VIR)
    return jax.shard_map(
        per_device,
        mesh=fine,
        in_specs=(
            P(VIR + OCC, None),
            P(VIR),
            P(VIR, None, None, OCC),
            P(VIR, None),
            P(),
        ),
        out_specs=P(VIR, OCC),
        check_vma=False,
    )
```

```python
import jax
import jax.numpy as jnp
from jax import lax
from jax.experimental import pallas as pl
from jax.experimental.pallas import tpu as pltpu
from jax.sharding import Mesh, PartitionSpec as P


OCC = ("zl", "x", "core")
VIR = ("zh", "y")
N_VIR = 32
N_X = 8
IRREPS = 8


def order_kernel(blocks_ref, panel_ref, out_ref):
    for slot in range(panel_ref.shape[0]):
        out_ref[blocks_ref[slot]] = panel_ref[slot]


def irrep_order(panel, blocks):
    return pl.pallas_call(
        order_kernel,
        out_shape=pltpu.VMEM(panel.shape, panel.dtype),
        in_specs=[
            pl.BlockSpec(memory_space=pltpu.SMEM),
            pl.BlockSpec(memory_space=pltpu.VMEM),
        ],
        out_specs=pl.BlockSpec(memory_space=pltpu.VMEM),
        name="irrep_order",
    )(blocks, panel)


def pick_kernel(owner_ref, pieces_ref, out_ref):
    count, rows, cols = pieces_ref.shape
    for step in range(out_ref.shape[1] // rows):
        out_ref[:, step * rows:(step + 1) * rows, :] = jnp.broadcast_to(
            pieces_ref[pl.ds(owner_ref[step], 1)], (count, rows, cols)
        )


def pick_and_copy(pieces, owners):
    count, rows, cols = pieces.shape
    return pl.pallas_call(
        pick_kernel,
        out_shape=pltpu.VMEM((count, owners.shape[0] * rows, cols), pieces.dtype),
        in_specs=[
            pl.BlockSpec(memory_space=pltpu.SMEM),
            pl.BlockSpec(memory_space=pltpu.VMEM),
        ],
        out_specs=pl.BlockSpec(memory_space=pltpu.VMEM),
    )(owners, pltpu.with_memory_space_constraint(pieces, pltpu.VMEM))


HERE, MINE, THEIRS = (0,), (1, 3), (-1, -3)
MIDDLE, OPPOSITE, OTHER_MIDDLE = (2,), (4,), (-2,)


def ladder_kernel(groups, piece_ref, second_ref, here_ref, side_ref, *refs):
    held_refs, refs = refs[:len(groups) - 1], refs[len(groups) - 1:]
    last_ref, weight_ref, out_ref, done_ref, sems, in_sems = refs[:6]
    tiles_refs = refs[6:]
    quarters = weight_ref.shape[0] // IRREPS
    copies = []
    arrivals = [
        pltpu.make_async_copy(held_ref, tiles_ref, in_sems.at[group])
        for group, (held_ref, tiles_ref) in enumerate(zip(held_refs, tiles_refs))
    ]
    for arrival in arrivals:
        arrival.start()
    side = 2 * side_ref[0] - 1
    for group, (steps, tiles_ref) in enumerate(zip(groups, (*tiles_refs, last_ref))):
        if group < len(arrivals):
            arrivals[group].wait()
        for index in range(tiles_ref.shape[0]):
            core, zl = index % 4 // 2, lax.rem(here_ref[1] + index % 2, 2)
            x = lax.rem((here_ref if group < 3 else second_ref)[0] + steps[index // 4] * side + N_X, N_X)
            tile = (zl * N_X + x) * 2 + core
            weights = weight_ref[pl.ds(piece_ref[tile], quarters)]
            rows = weights.shape[1] // 2
            weights = jnp.concatenate(
                [weights[:, :rows].reshape(-1, weights.shape[2]),
                 weights[:, rows:].reshape(-1, weights.shape[2])], axis=0)
            slot = len(copies)
            done_ref[slot] = jnp.dot(
                tiles_ref[index], weights, preferred_element_type=jnp.float32
            ).astype(done_ref.dtype)
            copy = pltpu.make_async_copy(done_ref.at[slot], out_ref.at[tile], sems.at[slot])
            copy.start()
            copies.append(copy)
    for copy in copies:
        copy.wait()


def contract(groups, arrays, first_piece, second, here, side, weights):
    rows = arrays[0].shape[1]
    cols = weights.shape[2]
    count = sum(array.shape[0] for array in arrays)
    vmem, smem = pl.BlockSpec(memory_space=pltpu.VMEM), pl.BlockSpec(memory_space=pltpu.SMEM)
    *arrays, last = arrays
    operands = [pltpu.with_memory_space_constraint(array, pltpu.HBM) for array in arrays]
    operands += [pltpu.with_memory_space_constraint(array, pltpu.VMEM) for array in (last, weights)]
    out = pl.pallas_call(
        lambda *refs: ladder_kernel(groups, *refs),
        out_shape=jax.ShapeDtypeStruct((count, rows, cols), jnp.bfloat16),
        in_specs=[smem] * 4 + [pl.BlockSpec(memory_space=pltpu.HBM)] * len(arrays) + [vmem] * 2,
        out_specs=pl.BlockSpec(memory_space=pl.ANY),
        scratch_shapes=[
            pltpu.VMEM((count, rows, cols), jnp.bfloat16),
            pltpu.SemaphoreType.DMA((count,)),
            pltpu.SemaphoreType.DMA((len(arrays),)),
            *(pltpu.VMEM(array.shape, array.dtype) for array in arrays),
        ],
        name="ladder",
    )(first_piece, second, here, side, *operands)
    return out.reshape(count * rows, cols)


def away(array, step):
    pairs = []
    for x in range(N_X):
        pairs.append((2 * x, 2 * ((x + step) % N_X)))
        pairs.append((2 * x + 1, 2 * ((x - step) % N_X) + 1))
    return lax.ppermute(array, ("x", "core"), pairs)


def per_device(amplitudes, pair_irrep, integrals, panel_blocks, panel_owner):
    cols = integrals.shape[-1]
    partner = lax.ppermute(amplitudes, "zl", [(0, 1), (1, 0)])
    ordered = irrep_order(integrals[0], panel_blocks[0])
    pieces = lax.all_to_all(ordered.reshape(N_VIR, -1, cols), VIR, 0, 0, tiled=True)
    pair = jnp.stack([amplitudes, partner])
    chip = lax.all_gather(pair, "core", axis=0, tiled=True)
    beside = away(chip, 1)
    three = away(chip, 3)
    here = jnp.stack([lax.axis_index("x"), lax.axis_index("zl")])
    copies = pick_and_copy(pieces, panel_owner)
    weights = lax.all_to_all(copies, VIR, 0, 0, tiled=True)
    side = jnp.arange(16, dtype=jnp.int32) + lax.axis_index("core")
    middle = away(beside, 1)
    opposite = away(three, 1)
    mine = jnp.concatenate([beside, three])
    theirs = lax.ppermute(mine, "core", [(0, 1), (1, 0)])
    second = jnp.arange(24, dtype=jnp.int32) + lax.axis_index("x")
    other_middle = lax.ppermute(middle, "core", [(0, 1), (1, 0)])
    first_piece = pair_irrep * (N_VIR // IRREPS)
    groups = (HERE, MINE, THEIRS, MIDDLE, OPPOSITE, OTHER_MIDDLE)
    arrays = (chip, mine, theirs, middle, opposite, other_middle)
    return contract(groups, arrays, first_piece, second, here, side, weights)


def solution(mesh):
    fine = Mesh(mesh.devices.reshape(2, 8, 2, 4, 8), OCC + VIR)
    return jax.shard_map(
        per_device,
        mesh=fine,
        in_specs=(
            P(VIR + OCC, None),
            P(VIR),
            P(VIR, None, None, OCC),
            P(VIR, None),
            P(),
        ),
        out_specs=P(VIR, OCC),
        check_vma=False,
    )
```

```python
import jax
import jax.numpy as jnp
from jax import lax
from jax.experimental import pallas as pl
from jax.experimental.pallas import tpu as pltpu
from jax.sharding import Mesh, PartitionSpec as P


OCC = ("zl", "x", "core")
VIR = ("zh", "y")
N_VIR = 32
N_X = 8
IRREPS = 8


def order_kernel(blocks_ref, panel_ref, out_ref):
    for slot in range(panel_ref.shape[0]):
        out_ref[blocks_ref[slot]] = panel_ref[slot]


def irrep_order(panel, blocks):
    return pl.pallas_call(
        order_kernel,
        out_shape=pltpu.VMEM(panel.shape, panel.dtype),
        in_specs=[
            pl.BlockSpec(memory_space=pltpu.SMEM),
            pl.BlockSpec(memory_space=pltpu.VMEM),
        ],
        out_specs=pl.BlockSpec(memory_space=pltpu.VMEM),
        name="irrep_order",
    )(blocks, panel)


def pick_kernel(owner_ref, pieces_ref, out_ref):
    count, rows, cols = pieces_ref.shape
    for step in range(out_ref.shape[1] // rows):
        out_ref[:, step * rows:(step + 1) * rows, :] = jnp.broadcast_to(
            pieces_ref[pl.ds(owner_ref[step], 1)], (count, rows, cols)
        )


def pick_and_copy(pieces, owners):
    count, rows, cols = pieces.shape
    return pl.pallas_call(
        pick_kernel,
        out_shape=pltpu.VMEM((count, owners.shape[0] * rows, cols), pieces.dtype),
        in_specs=[
            pl.BlockSpec(memory_space=pltpu.SMEM),
            pl.BlockSpec(memory_space=pltpu.VMEM),
        ],
        out_specs=pl.BlockSpec(memory_space=pltpu.VMEM),
    )(owners, pltpu.with_memory_space_constraint(pieces, pltpu.VMEM))


HERE, MINE, THEIRS = (0,), (1, 2), (-1, -2)
THIRD, OPPOSITE, OTHER_THIRD = (3,), (4,), (-3,)


def ladder_kernel(groups, piece_ref, second_ref, here_ref, side_ref, *refs):
    held_refs, refs = refs[:len(groups) - 1], refs[len(groups) - 1:]
    last_ref, weight_ref, out_ref, done_ref, sems, in_sems = refs[:6]
    tiles_refs = refs[6:]
    quarters = weight_ref.shape[0] // IRREPS
    copies = []
    arrivals = [
        pltpu.make_async_copy(held_ref, tiles_ref, in_sems.at[group])
        for group, (held_ref, tiles_ref) in enumerate(zip(held_refs, tiles_refs))
    ]
    for arrival in arrivals:
        arrival.start()
    side = 2 * side_ref[0] - 1
    for group, (steps, tiles_ref) in enumerate(zip(groups, (*tiles_refs, last_ref))):
        if group < len(arrivals):
            arrivals[group].wait()
        for index in range(tiles_ref.shape[0]):
            core, zl = index % 4 // 2, lax.rem(here_ref[1] + index % 2, 2)
            x = lax.rem((here_ref if group < 3 else second_ref)[0] + steps[index // 4] * side + N_X, N_X)
            tile = (zl * N_X + x) * 2 + core
            weights = weight_ref[pl.ds(piece_ref[tile], quarters)]
            rows = weights.shape[1] // 2
            weights = jnp.concatenate(
                [weights[:, :rows].reshape(-1, weights.shape[2]),
                 weights[:, rows:].reshape(-1, weights.shape[2])], axis=0)
            slot = len(copies)
            done_ref[slot] = jnp.dot(
                tiles_ref[index], weights, preferred_element_type=jnp.float32
            ).astype(done_ref.dtype)
            copy = pltpu.make_async_copy(done_ref.at[slot], out_ref.at[tile], sems.at[slot])
            copy.start()
            copies.append(copy)
    for copy in copies:
        copy.wait()


def contract(groups, arrays, first_piece, second, here, side, weights):
    rows = arrays[0].shape[1]
    cols = weights.shape[2]
    count = sum(array.shape[0] for array in arrays)
    vmem, smem = pl.BlockSpec(memory_space=pltpu.VMEM), pl.BlockSpec(memory_space=pltpu.SMEM)
    *arrays, last = arrays
    operands = [pltpu.with_memory_space_constraint(array, pltpu.HBM) for array in arrays]
    operands += [pltpu.with_memory_space_constraint(array, pltpu.VMEM) for array in (last, weights)]
    out = pl.pallas_call(
        lambda *refs: ladder_kernel(groups, *refs),
        out_shape=jax.ShapeDtypeStruct((count, rows, cols), jnp.bfloat16),
        in_specs=[smem] * 4 + [pl.BlockSpec(memory_space=pltpu.HBM)] * len(arrays) + [vmem] * 2,
        out_specs=pl.BlockSpec(memory_space=pl.ANY),
        scratch_shapes=[
            pltpu.VMEM((count, rows, cols), jnp.bfloat16),
            pltpu.SemaphoreType.DMA((count,)),
            pltpu.SemaphoreType.DMA((len(arrays),)),
            *(pltpu.VMEM(array.shape, array.dtype) for array in arrays),
        ],
        name="ladder",
    )(first_piece, second, here, side, *operands)
    return out.reshape(count * rows, cols)


def away(array, step):
    pairs = []
    for x in range(N_X):
        pairs.append((2 * x, 2 * ((x + step) % N_X)))
        pairs.append((2 * x + 1, 2 * ((x - step) % N_X) + 1))
    return lax.ppermute(array, ("x", "core"), pairs)


def per_device(amplitudes, pair_irrep, integrals, panel_blocks, panel_owner):
    cols = integrals.shape[-1]
    partner = lax.ppermute(amplitudes, "zl", [(0, 1), (1, 0)])
    ordered = irrep_order(integrals[0], panel_blocks[0])
    pieces = lax.all_to_all(ordered.reshape(N_VIR, -1, cols), VIR, 0, 0, tiled=True)
    pair = jnp.stack([amplitudes, partner])
    chip = lax.all_gather(pair, "core", axis=0, tiled=True)
    beside = away(chip, 1)
    two = away(chip, 2)
    here = jnp.stack([lax.axis_index("x"), lax.axis_index("zl")])
    copies = pick_and_copy(pieces, panel_owner)
    weights = lax.all_to_all(copies, VIR, 0, 0, tiled=True)
    side = jnp.arange(16, dtype=jnp.int32) + lax.axis_index("core")
    opposite = away(two, 2)
    third = away(two, 1)
    mine = jnp.concatenate([beside, two])
    theirs = lax.ppermute(mine, "core", [(0, 1), (1, 0)])
    second = jnp.arange(24, dtype=jnp.int32) + lax.axis_index("x")
    other_third = lax.ppermute(third, "core", [(0, 1), (1, 0)])
    first_piece = pair_irrep * (N_VIR // IRREPS)
    groups = (HERE, MINE, THEIRS, THIRD, OPPOSITE, OTHER_THIRD)
    arrays = (chip, mine, theirs, third, opposite, other_third)
    return contract(groups, arrays, first_piece, second, here, side, weights)


def solution(mesh):
    fine = Mesh(mesh.devices.reshape(2, 8, 2, 4, 8), OCC + VIR)
    return jax.shard_map(
        per_device,
        mesh=fine,
        in_specs=(
            P(VIR + OCC, None),
            P(VIR),
            P(VIR, None, None, OCC),
            P(VIR, None),
            P(),
        ),
        out_specs=P(VIR, OCC),
        check_vma=False,
    )
```
